32 devices in a mesh: groups: 2 (over y), vocab: 4 (over z), tokens: 2 (over x), section: 2 (over core).
Axes of the slice: x: 2, y: 2, z: 4, core: 2. Of those that a mesh axis runs over, the one named last changes fastest.
Arguments:
- teacher_hidden: bfloat16 [512, 16384], P(('groups', 'vocab', 'section'), 'tokens'), parts along dimension 0
- teacher_weight: bfloat16 [16384, 4096], P('tokens', ('vocab', 'section'))
- student_hidden: bfloat16 [512, 4096], P(('groups', 'tokens')), parts along dimension 0
- student_gain: float32 [4096], replicated, may hold values from 0.5 to 1.5
- student_weight: bfloat16 [4096, 4096], P('tokens', ('vocab', 'section'))
- labels: int32 [512], P(('groups', 'tokens')), parts along dimension 0, may hold values from 0 to 4095
- alignment: int32 [512], P(('groups', 'tokens')), parts along dimension 0, may hold values from 0 to 255, as said below
- loss_mask: int32 [512], P('groups'), parts along dimension 0, may hold values from 0 to 1, as said below
Outputs:
- row_loss: float32 [512], P(('groups', 'tokens')), parts along dimension 0
- logit_grad: bfloat16 [512, 4096], P(('groups', 'tokens'), ('vocab', 'section')), parts along dimension 0
- hidden_grad: bfloat16 [512, 4096], P(('groups', 'tokens'), ('vocab', 'section')), parts along dimension 0
The draws below stay inside these ranges and needn't reach their ends.
There are 2 independent parts, one for each index of `groups`. The reference program is written for one: setup_inputs(seed, part) draws one part's arguments, and reference() takes and returns one part's arrays. A program takes and returns all parts, laid end to end along the dimension named above; an argument that names none is the same for every part. Nothing has to cross between parts.
Inputs may be any that keep to these rules, and one draw needn't show every extreme that they name: Within each aligned block of 128 frames the alignment never falls, names only tokens of the same block, and starts at the block's first token and ends at its last. `loss_mask`: the last frame always counts.
All inputs are finite; a program needn't handle non-finite values.
Results may differ from the reference program's by a relative error of at most 0.0061.
Values may be sent and summed in bfloat16 or wider, within the bound.
A program may use at most 64 MiB of HBM per device.

```python
import math
import jax
import jax.numpy as jnp
from jax import lax

DT = 16384
DS = 4096
TOK_DEV = 128
TOK = 256
V = 4096


def drawn_values(key, rows, width, factor):
    return jnp.clip(jax.random.normal(key, (rows, width), jnp.float32), -5.0, 5.0) * factor


def draw_teacher_hidden(key, part):
    own_key = jax.random.fold_in(key, 101)
    values = drawn_values(own_key, TOK, DT, 1.0)
    return values.astype(jnp.bfloat16)


def draw_student_hidden(key, part):
    own_key = jax.random.fold_in(key, 202)
    values = drawn_values(own_key, TOK, DS, 1.0)
    return values.astype(jnp.bfloat16)


def draw_teacher_weight(key, part):
    own_key = jax.random.fold_in(key, 303)
    values = drawn_values(own_key, DT, V, 3.0 / math.sqrt(DT))
    return values.astype(jnp.bfloat16)


def draw_student_weight(key, part):
    own_key = jax.random.fold_in(key, 404)
    values = drawn_values(own_key, DS, V, 3.0 / math.sqrt(DS))
    return values.astype(jnp.bfloat16)


def draw_alignment(key, part):
    blocks = TOK // TOK_DEV
    offsets = jnp.sort(jax.random.randint(key, (blocks, TOK_DEV), 0, TOK_DEV), axis=1)
    position = jnp.arange(TOK_DEV, dtype=jnp.int32)[None, :]
    offsets = jnp.where(position == 0, 0, jnp.where(position == TOK_DEV - 1, TOK_DEV - 1, offsets))
    starts = jnp.arange(blocks, dtype=jnp.int32)[:, None] * TOK_DEV
    return (starts + offsets).reshape(TOK).astype(jnp.int32)


def draw_loss_mask(key, part):
    values = jax.random.randint(key, (TOK,), 0, 3 * TOK - 3)
    limits = 3 * jnp.arange(TOK, dtype=jnp.int32)
    return (values < limits).astype(jnp.int32)


def touch_ends(entries, stream_key, low, top_value):
    shape = entries.shape
    index_at = [jax.random.randint(jax.random.fold_in(stream_key, axis), (), 0, shape[axis]) for axis in range(len(shape))]
    entries = entries.at[tuple(index_at)].set(low)
    longest = shape.index(max(shape))
    index_at[longest] = (index_at[longest] + 1) % shape[longest]
    return entries.at[tuple(index_at)].set(top_value)


def setup_inputs(seed: int = 0, part: int = 0) -> dict:
    arg_keys = jax.random.split(jax.random.key(seed), 9)
    part_keys = jax.random.split(jax.random.fold_in(arg_keys[8], part), 9)
    return {
        "teacher_hidden": draw_teacher_hidden(jax.random.fold_in(jax.random.fold_in(arg_keys[8], part), 71), part),
        "teacher_weight": draw_teacher_weight(jax.random.fold_in(arg_keys[8], 71), part),
        "student_hidden": draw_student_hidden(jax.random.fold_in(jax.random.fold_in(arg_keys[8], part), 71), part),
        "student_gain": jnp.clip(1.0 + 0.1 * jax.random.normal(arg_keys[3], (DS,), jnp.float32), 0.5, 1.5),
        "student_weight": draw_student_weight(jax.random.fold_in(arg_keys[8], 71), part),
        "labels": touch_ends(jax.random.randint(part_keys[5], (TOK,), 0, V), jax.random.fold_in(part_keys[5], 1), 0, V - 1).astype(jnp.int32),
        "alignment": draw_alignment(jax.random.fold_in(jax.random.fold_in(arg_keys[8], part), 71), part),
        "loss_mask": draw_loss_mask(jax.random.fold_in(jax.random.fold_in(arg_keys[8], part), 71), part),
    }


label_weight = 0.2
loss_scale = 16.0
epsilon = 1e-05

def reference(teacher_hidden, teacher_weight, student_hidden, student_gain, student_weight, labels, alignment, loss_mask):
    aligned = jnp.dot(teacher_hidden[alignment], teacher_weight, preferred_element_type=jnp.float32)
    hidden = student_hidden.astype(jnp.float32)
    inverse = lax.rsqrt(lax.optimization_barrier(jnp.mean(hidden * hidden, axis=1, keepdims=True)) + epsilon)
    normed = (hidden * inverse * student_gain).astype(jnp.bfloat16)
    student = jnp.dot(normed, student_weight, preferred_element_type=jnp.float32)
    lse_t = jax.nn.logsumexp(aligned, axis=1)
    lse_s = jax.nn.logsumexp(student, axis=1)
    teacher_prob = jnp.exp(aligned - lse_t[:, None])
    student_prob = jnp.exp(student - lse_s[:, None])
    diverge = lax.optimization_barrier(jnp.sum(teacher_prob * (aligned - student), axis=1)) - lse_t + lse_s
    onehot = labels[:, None] == jnp.arange(student.shape[1], dtype=jnp.int32)[None, :]
    label_logit = lax.optimization_barrier(jnp.sum(jnp.where(onehot, student, 0.0), axis=1))
    cross_term = lse_s - label_logit
    mask_float = loss_mask.astype(jnp.float32)
    mask_count = jnp.sum(mask_float)
    row_weight = mask_float * loss_mask.shape[0] / mask_count
    row_loss = row_weight * (diverge + label_weight * cross_term)
    onehot_float = onehot.astype(jnp.float32)
    logit_grad = (loss_scale * row_weight[:, None] * ((1.0 + label_weight) * student_prob - teacher_prob - label_weight * onehot_float)).astype(jnp.bfloat16)
    normed_grad = jnp.dot(logit_grad, student_weight.T, preferred_element_type=jnp.float32)
    scaled = normed_grad * student_gain
    inner_rows = lax.optimization_barrier(jnp.sum(scaled * hidden, axis=1, keepdims=True))
    hidden_grad = (inverse * scaled - hidden * inverse ** 3 * inner_rows / hidden.shape[1]).astype(jnp.bfloat16)
    return (row_loss, logit_grad, hidden_grad)
```

```python
import functools

import jax
import jax.numpy as jnp
from jax import lax
from jax.experimental import pallas as pl
from jax.experimental.pallas import tpu as pltpu
from jax.sharding import PartitionSpec as P

label_weight = 0.2
loss_scale = 16.0
epsilon = 1e-05
MESH = pl.DeviceIdType.MESH


def kernel(
    sizes, th, tw, sh, gain, sw, labels, align, mask,
    rl_out, lg_out, hg_out,
    tbuf, twv, wbuf, normed, acc, tin, bl, stats, inner_in, sibout, sibin, part, rin, lin, inner_acc,
    tw_sem, own_sem, sw_sem,
    left_send, right_send, sib_send, z_recv, s_recv,
    x_send, x_recv, y_send, y_recv,
    acc_send, acc_recv,
    stat_send, stat_recv, inner_send, inner_recv,
    gs_send, gs_recv, ln_send, r_recv, l_recv,
):
    G, V, T, S, C, CW = sizes
    VS = V * S
    g, v, t, s = (lax.axis_index(a) for a in ("groups", "vocab", "tokens", "section"))
    me = v * S + s
    rows = th.shape[0]
    fc = th.shape[1] // C
    F = sw.shape[0]
    half = F // 2
    wc = half // CW
    frames, DS = sh.shape
    N = tw.shape[1]
    w = DS // VS
    per = V // T

    def did(gg=None, vv=None, tt=None, ss=None):
        pick = lambda a, b: b if a is None else a
        return (pick(gg, g), pick(vv, v), pick(tt, t), pick(ss, s))

    def remote(src, dst, send, recv, where):
        return pltpu.make_async_remote_copy(
            src_ref=src, dst_ref=dst, send_sem=send, recv_sem=recv,
            device_id=where, device_id_type=MESH,
        )

    def vs_peer(k):
        other = lax.rem(me + k, VS)
        return did(vv=other // S, ss=lax.rem(other, S)), other

    def each(lo, hi, body):
        def run(i, carry):
            body(i)
            return carry
        lax.fori_loop(lo, hi, run, 0)

    barrier = pltpu.get_barrier_semaphore()

    def greet(where):
        pl.semaphore_signal(barrier, inc=1, device_id=where, device_id_type=MESH)

    for c in range(C):
        pltpu.make_async_copy(tw.at[c * fc:(c + 1) * fc], twv.at[c], tw_sem.at[c]).start()
        pltpu.make_async_copy(th.at[:, c * fc:(c + 1) * fc], tbuf.at[c, me], own_sem.at[c]).start()
    sw_copy = pltpu.make_async_copy(sw, wbuf.at[pl.ds(pl.multiple_of(t * F, F), F)], sw_sem)
    sw_copy.start()

    each(1, VS, lambda k: greet(vs_peer(k)[0]))
    each(1, T, lambda k: greet(did(tt=lax.rem(t + k, T))))
    greet(did(gg=1 - g))
    pl.semaphore_wait(barrier, VS - 1 + T - 1 + 1)

    def go_left(o, c, src):
        return remote(src, tbuf.at[c, o * S + s], left_send.at[o, c], z_recv.at[o, c], did(vv=v - 1))

    def go_right(o, c, src):
        return remote(src, tbuf.at[c, o * S + s], right_send.at[o, c], z_recv.at[o, c], did(vv=v + 1))

    def go_sib(o, c, src):
        return remote(src, tbuf.at[c, o * S + s], sib_send.at[o, c], s_recv.at[o, c], did(ss=1 - s))

    for c in range(C):
        own = th.at[:, c * fc:(c + 1) * fc]

        @pl.when(v > 0)
        def _():
            go_left(v, c, own).start()

        @pl.when(v < V - 1)
        def _():
            go_right(v, c, own).start()

    def w_at(tt, hh, cw):
        return wbuf.at[pl.ds(pl.multiple_of(tt * F + hh * half + cw * wc, wc), wc)]

    def go_x(k, cw):
        to = lax.rem(t + k, T)
        src = sw.at[pl.ds(pl.multiple_of(g * half + cw * wc, wc), wc)]
        return remote(src, w_at(t, g, cw), x_send.at[to, cw], x_recv.at[t, cw], did(tt=to))

    def go_y(tt, cw):
        return remote(w_at(tt, g, cw), w_at(tt, g, cw), y_send.at[tt, cw], y_recv.at[tt, cw], did(gg=1 - g))

    def x_wait(tt, cw):
        remote(w_at(tt, g, cw), w_at(tt, g, cw), x_send.at[tt, cw], x_recv.at[tt, cw], did(tt=tt)).wait_recv()

    def y_wait(tt, cw):
        remote(w_at(tt, 1 - g, cw), w_at(tt, 1 - g, cw), y_send.at[tt, cw], y_recv.at[tt, cw], did(gg=1 - g)).wait_recv()

    nev = (T - 1) * CW
    each(0, nev, lambda j: go_x(j // CW + 1, lax.rem(j, CW)).start())
    for c in range(C):
        go_sib(v, c, th.at[:, c * fc:(c + 1) * fc]).start()

    def pass_on(j):
        tt = lax.rem(t + T - 1 - j // CW, T)
        cw = lax.rem(j, CW)
        x_wait(tt, cw)
        go_y(tt, cw).start()

    hid = sh[...].astype(jnp.float32)
    inverse = lax.rsqrt(jnp.mean(hid * hid, axis=1, keepdims=True) + epsilon)
    normed[...] = (hid * inverse * gain[...]).astype(jnp.bfloat16)

    def multiply(o, c):
        x = tbuf[c, pl.ds(o * S, S)].reshape(S * rows, fc)
        acc[o] += jnp.dot(x, twv[c], preferred_element_type=jnp.float32)

    def go_acc(o):
        to = o // per
        return remote(acc.at[o], tin.at[t, lax.rem(o, per)], acc_send.at[o], acc_recv.at[t, lax.rem(o, per)], did(tt=to))

    def finished(o):
        @pl.when(o // per != t)
        def _():
            go_acc(o).start()

    acc[...] = jnp.zeros_like(acc)

    def own_chunk(c):
        pltpu.make_async_copy(tbuf.at[c, me], tbuf.at[c, me], own_sem.at[c]).wait()
        pltpu.make_async_copy(twv.at[c], twv.at[c], tw_sem.at[c]).wait()
        other = tbuf.at[c, v * S + 1 - s]
        remote(other, other, sib_send.at[v, c], s_recv.at[v, c], did(ss=1 - s)).wait_recv()
        multiply(v, c)

    each(0, C, own_chunk)
    finished(v)

    def take(o, c, onward, has_next):
        here = tbuf.at[c, o * S + s]
        remote(here, here, sib_send.at[o, c], z_recv.at[o, c], did(ss=1 - s)).wait_recv()

        @pl.when(has_next)
        def _():
            onward(o, c, here).start()

        go_sib(o, c, here).start()

    def use(o, c):
        other = tbuf.at[c, o * S + 1 - s]
        remote(other, other, sib_send.at[o, c], s_recv.at[o, c], did(ss=1 - s)).wait_recv()
        multiply(o, c)

        @pl.when(c == C - 1)
        def _():
            finished(o)

    steps = (V - 1) * C
    stride = max(1, (steps - 2) // nev)

    def step(i):
        k, c = i // C + 1, lax.rem(i, C)

        @pl.when(i < steps)
        def _():
            @pl.when(v + k < V)
            def _():
                take(v + k, c, go_left, v > 0)

            @pl.when(v - k >= 0)
            def _():
                take(v - k, c, go_right, v < V - 1)

        j = i // stride - 1

        @pl.when((lax.rem(i, stride) == 0) & (j >= 0) & (j < nev))
        def _():
            pass_on(j)

        @pl.when(i > 0)
        def _():
            kk, cc = (i - 1) // C + 1, lax.rem(i - 1, C)

            @pl.when(v + kk < V)
            def _():
                use(v + kk, cc)

            @pl.when(v - kk >= 0)
            def _():
                use(v - kk, cc)

    each(0, steps + 1, step)
    each(min(nev, steps // stride), nev, pass_on)

    sw_copy.wait()

    def y_in(j):
        y_wait(lax.rem(t + T - 1 - j // CW, T), lax.rem(j, CW))

    each(0, nev, y_in)
    student = jnp.dot(normed[...], wbuf[...], preferred_element_type=jnp.float32)
    lane_n = lax.broadcasted_iota(jnp.int32, (frames, N), 1)
    lane = lax.broadcasted_iota(jnp.int32, (frames, frames), 1)
    sub = lax.broadcasted_iota(jnp.int32, (frames, frames), 0)

    def to_columns(row):
        return jnp.transpose(jnp.broadcast_to(row, (frames, frames)))

    label_col = to_columns(labels[...].astype(jnp.float32)).astype(jnp.int32)[:, 0:1]
    onehot = (label_col - me * N) == lane_n
    label_logit = jnp.sum(jnp.where(onehot, student, 0.0), axis=1, keepdims=True)
    top_s = jnp.max(student, axis=1, keepdims=True)
    sum_s = jnp.sum(jnp.exp(student - top_s), axis=1, keepdims=True)
    align_cols = to_columns(align[...].astype(jnp.float32)).astype(jnp.int32) - t * frames
    pick = (align_cols == lane).astype(jnp.bfloat16)

    def tin_wait(j):
        tt, p = lax.rem(t + 1 + j // per, T), lax.rem(j, per)
        remote(tin.at[tt, p], tin.at[tt, p], acc_send.at[0], acc_recv.at[tt, p], did(tt=tt)).wait_recv()

    each(0, (T - 1) * per, tin_wait)
    for p in range(per):
        total = acc[t * per + p]
        for k in range(1, T):
            total = total + tin[lax.rem(t + k, T), p]
        bl[p * S * rows:(p + 1) * S * rows, :] = total
    whole = bl[...]
    hi = whole.astype(jnp.bfloat16)
    rest = whole - hi.astype(jnp.float32)
    mid = rest.astype(jnp.bfloat16)
    low = (rest - mid.astype(jnp.float32)).astype(jnp.bfloat16)
    rows_of = lambda piece: jnp.dot(pick, piece, preferred_element_type=jnp.float32)
    aligned = (rows_of(low) + rows_of(mid)) + rows_of(hi)
    top_t = jnp.max(aligned, axis=1, keepdims=True)
    exp_t = jnp.exp(aligned - top_t)
    sum_t = jnp.sum(exp_t, axis=1, keepdims=True)
    cross_t = jnp.sum(exp_t * (aligned - student), axis=1, keepdims=True)

    packed = jnp.zeros((frames, frames), jnp.float32)
    for i, column in enumerate((top_t, sum_t, cross_t, top_s, sum_s, label_logit)):
        packed = jnp.where(lane == i, column, packed)
    stats[me] = jnp.transpose(packed)[0:8, :]

    def go_stat(k):
        where, other = vs_peer(k)
        return remote(stats.at[me], stats.at[me], stat_send.at[other], stat_recv.at[me], where)

    each(1, VS, lambda k: go_stat(k).start())

    def stat_wait(k):
        where, other = vs_peer(k)
        remote(stats.at[other], stats.at[other], stat_send.at[other], stat_recv.at[other], where).wait_recv()

    each(1, VS, stat_wait)
    st = stats[...]
    row = lambda i: st[:, i, :]
    all_t = jnp.max(row(0), axis=0, keepdims=True)
    all_s = jnp.max(row(3), axis=0, keepdims=True)
    scale_t = jnp.exp(row(0) - all_t)
    scale_s = jnp.exp(row(3) - all_s)
    add = lambda x: jnp.sum(x, axis=0, keepdims=True)
    total_t = add(row(1) * scale_t)
    lse_t = all_t + jnp.log(total_t)
    lse_s = all_s + jnp.log(add(row(4) * scale_s))
    diverge = add(row(2) * scale_t) / total_t - lse_t + lse_s
    cross_term = lse_s - add(row(5))
    mask_float = mask[...].astype(jnp.float32)
    mask_count = jnp.sum(jnp.sum(mask_float, axis=1, keepdims=True), axis=0, keepdims=True)
    own_mask = mask[pl.ds(t, 1), :].astype(jnp.float32)
    row_weight = own_mask * (T * frames) / mask_count
    rl_out[...] = row_weight * (diverge + label_weight * cross_term)

    unpacked = jnp.where(sub == 0, lse_t, jnp.where(sub == 1, lse_s, row_weight))
    columns = jnp.transpose(unpacked)
    teacher_prob = jnp.exp(aligned - columns[:, 0:1])
    student_prob = jnp.exp(student - columns[:, 1:2])
    grad = (
        loss_scale * columns[:, 2:3]
        * ((1.0 + label_weight) * student_prob - teacher_prob - label_weight * onehot.astype(jnp.float32))
    ).astype(jnp.bfloat16)
    lg_out[...] = grad

    inner_acc[...] = jnp.zeros_like(inner_acc)

    def term(block):
        at = pl.multiple_of(block * w, w)
        value = lax.dot_general(
            lg_out[...], wbuf[pl.ds(at, w), :], (((1,), (1,)), ((), ())), preferred_element_type=jnp.float32
        )
        weighted = value * gain[:, pl.ds(at, w)] * sh[:, pl.ds(at, w)].astype(jnp.float32)
        inner_acc[...] += jnp.sum(weighted, axis=1, keepdims=True)
        return value

    def go_gs(b):
        return remote(sibout.at[b], sibin.at[b], gs_send.at[b], gs_recv.at[b], did(ss=1 - s))

    def order(q):
        return lax.rem(q, 2) * (q // 2) + (1 - lax.rem(q, 2)) * (V - 1 - q // 2)

    def for_sib(q):
        b = order(q)
        sibout[b] = term(b * S + 1 - s)
        go_gs(b).start()

    def for_own(q):
        b = order(q)
        part[b] = term(b * S + s)

    each(0, V, for_sib)
    each(0, V, for_own)
    inner_in[me] = jnp.transpose(jnp.broadcast_to(inner_acc[...], (frames, frames)))[0:8, :]

    def go_inner(k):
        where, other = vs_peer(k)
        return remote(inner_in.at[me], inner_in.at[me], inner_send.at[other], inner_recv.at[me], where)

    each(1, VS, lambda k: go_inner(k).start())

    def line(buf, recv, b, comes, onward):
        go_gs(b).wait_recv()
        part[b] += sibin[b]

        @pl.when(comes)
        def _():
            remote(part.at[b], buf.at[b], ln_send.at[b], recv.at[b], did(vv=onward)).wait_recv()
            part[b] += buf[b]

        remote(part.at[b], buf.at[b], ln_send.at[b], recv.at[b], did(vv=onward)).start()

    def line_step(q):
        b = V - 1 - q

        @pl.when(b > v)
        def _():
            line(rin, r_recv, b, v > 0, v + 1)

        @pl.when(q < v)
        def _():
            line(lin, l_recv, q, v < V - 1, v - 1)

    each(0, V - 1, line_step)

    def inner_wait(k):
        where, other = vs_peer(k)
        remote(inner_in.at[other], inner_in.at[other], inner_send.at[other], inner_recv.at[other], where).wait_recv()

    each(1, VS, inner_wait)
    inner_total = jnp.sum(inner_in[...], axis=0)[0:1, :]
    inner_rows = to_columns(inner_total)[:, 0:1]

    go_gs(v).wait_recv()
    part[v] += sibin[v]

    @pl.when(v > 0)
    def _():
        remote(part.at[v], rin.at[v], ln_send.at[v], r_recv.at[v], did(vv=v - 1)).wait_recv()
        part[v] += rin[v]

    @pl.when(v < V - 1)
    def _():
        remote(part.at[v], lin.at[v], ln_send.at[v], l_recv.at[v], did(vv=v + 1)).wait_recv()
        part[v] += lin[v]

    mine = pl.multiple_of(me * w, w)
    scaled = part[v] * gain[:, pl.ds(mine, w)]
    own_hidden = sh[:, pl.ds(mine, w)].astype(jnp.float32)
    hg_out[...] = (inverse * scaled - own_hidden * (inverse**3 * inner_rows / DS)).astype(jnp.bfloat16)

    def sent(i):
        o, c = i // C, lax.rem(i, C)
        here = tbuf.at[c, o * S + s]

        @pl.when((o >= v) & (v > 0))
        def _():
            go_left(o, c, here).wait_send()

        @pl.when((o <= v) & (v < V - 1))
        def _():
            go_right(o, c, here).wait_send()

        go_sib(o, c, here).wait_send()

    each(0, V * C, sent)

    def w_sent(j):
        go_x(j // CW + 1, lax.rem(j, CW)).wait_send()
        go_y(lax.rem(t + T - 1 - j // CW, T), lax.rem(j, CW)).wait_send()

    each(0, nev, w_sent)

    def acc_sent(o):
        @pl.when(o // per != t)
        def _():
            go_acc(o).wait_send()

        go_gs(o).wait_send()

        @pl.when(o > v)
        def _():
            remote(part.at[o], rin.at[o], ln_send.at[o], r_recv.at[o], did(vv=v + 1)).wait_send()

        @pl.when(o < v)
        def _():
            remote(part.at[o], lin.at[o], ln_send.at[o], l_recv.at[o], did(vv=v - 1)).wait_send()

    each(0, V, acc_sent)

    def small_sent(k):
        go_stat(k).wait_send()
        go_inner(k).wait_send()

    each(1, VS, small_sent)


def local(sizes, teacher_hidden, teacher_weight, student_hidden, student_gain, student_weight, labels, alignment, loss_mask):
    G, V, T, S, C, CW = sizes
    VS = V * S
    rows, width = teacher_hidden.shape
    fc = width // C
    N = teacher_weight.shape[1]
    frames, DS = student_hidden.shape
    w = DS // VS
    per = V // T
    f32, bf16 = jnp.float32, jnp.bfloat16
    dma = pltpu.SemaphoreType.DMA
    vmem = pl.BlockSpec(memory_space=pltpu.VMEM)
    hbm = pl.BlockSpec(memory_space=pl.ANY)
    row_loss, logit_grad, hidden_grad = pl.pallas_call(
        functools.partial(kernel, sizes),
        out_shape=(
            jax.ShapeDtypeStruct((1, frames), f32),
            jax.ShapeDtypeStruct((frames, N), bf16),
            jax.ShapeDtypeStruct((frames, w), bf16),
        ),
        in_specs=[hbm, hbm, vmem, vmem, hbm, vmem, vmem, vmem],
        out_specs=(vmem, vmem, vmem),
        scratch_shapes=[
            pltpu.VMEM((C, VS, rows, fc), bf16),
            pltpu.VMEM((C, fc, N), bf16),
            pltpu.VMEM((DS, N), bf16),
            pltpu.VMEM((frames, DS), bf16),
            pltpu.VMEM((V, S * rows, N), f32),
            pltpu.VMEM((T, per, S * rows, N), f32),
            pltpu.VMEM((frames, N), f32),
            pltpu.VMEM((VS, 8, frames), f32),
            pltpu.VMEM((VS, 8, frames), f32),
            pltpu.VMEM((V, frames, w), f32),
            pltpu.VMEM((V, frames, w), f32),
            pltpu.VMEM((V, frames, w), f32),
            pltpu.VMEM((V, frames, w), f32),
            pltpu.VMEM((V, frames, w), f32),
            pltpu.VMEM((frames, 1), f32),
            dma((C,)), dma((C,)), dma,
            dma((V, C)), dma((V, C)), dma((V, C)), dma((V, C)), dma((V, C)),
            dma((T, CW)), dma((T, CW)), dma((T, CW)), dma((T, CW)),
            dma((V,)), dma((T, per)),
            dma((VS,)), dma((VS,)), dma((VS,)), dma((VS,)),
            dma((V,)), dma((V,)), dma((V,)), dma((V,)), dma((V,)),
        ],
        compiler_params=pltpu.CompilerParams(
            collective_id=0, has_side_effects=True, vmem_limit_bytes=48 * 2**20
        ),
    )(
        teacher_hidden, teacher_weight, student_hidden, student_gain.reshape(1, DS), student_weight,
        labels.reshape(1, frames), alignment.reshape(1, frames), loss_mask.reshape(T, frames),
    )
    return row_loss.reshape(frames), logit_grad, hidden_grad


def solution(mesh):
    sizes = tuple(mesh.shape[a] for a in ("groups", "vocab", "tokens", "section")) + (4, 4)
    in_specs = (
        P(("groups", "vocab", "section"), "tokens"),
        P("tokens", ("vocab", "section")),
        P(("groups", "tokens"), None),
        P(),
        P("tokens", ("vocab", "section")),
        P(("groups", "tokens")),
        P(("groups", "tokens")),
        P("groups"),
    )
    out_specs = (
        P(("groups", "tokens")),
        P(("groups", "tokens"), ("vocab", "section")),
        P(("groups", "tokens"), ("vocab", "section")),
    )
    return jax.shard_map(
        functools.partial(local, sizes), mesh=mesh, in_specs=in_specs, out_specs=out_specs, check_vma=False
    )
```

```python
import functools

import jax
import jax.numpy as jnp
from jax import lax
from jax.experimental import pallas as pl
from jax.experimental.pallas import tpu as pltpu
from jax.sharding import PartitionSpec as P

label_weight = 0.2
loss_scale = 16.0
epsilon = 1e-05
MESH = pl.DeviceIdType.MESH


def kernel(
    sizes, th, tw, sh_in, gain_in, sw, labels_in, align_in, mask_in,
    rl_hbm, lg_hbm, hg_hbm,
    sh, gain, labels, align, mask, rl_out, lg_out, hg_out,
    tbuf, twv, wbuf, normed, acc, tin, bl, stats, inner_in, sibout, sibin, part, rin, lin, inner_acc,
    tw_sem, own_sem, sw_sem, in_sem, out_sem,
    left_send, right_send, sib_send, z_recv, s_recv,
    x_send, x_recv, y_send, y_recv,
    acc_send, acc_recv,
    stat_send, stat_recv, inner_send, inner_recv,
    gs_send, gs_recv, ln_send, r_recv, l_recv,
):
    G, V, T, S, C, CW, RP, WIN, LAG = sizes
    VS = V * S
    g, v, t, s = (lax.axis_index(a) for a in ("groups", "vocab", "tokens", "section"))
    me = v * S + s
    rows = th.shape[0]
    fc = th.shape[1] // C
    F = sw.shape[0]
    half = F // 2
    wc = half // CW
    frames, DS = sh.shape
    N = tw.shape[1]
    w = DS // VS
    per = V // T
    rp = frames // RP

    def did(gg=None, vv=None, tt=None, ss=None):
        pick = lambda a, b: b if a is None else a
        return (pick(gg, g), pick(vv, v), pick(tt, t), pick(ss, s))

    def remote(src, dst, send, recv, where):
        return pltpu.make_async_remote_copy(
            src_ref=src, dst_ref=dst, send_sem=send, recv_sem=recv,
            device_id=where, device_id_type=MESH,
        )

    def vs_peer(k):
        other = lax.rem(me + k, VS)
        return did(vv=other // S, ss=lax.rem(other, S)), other

    def each(lo, hi, body):
        def run(i, carry):
            body(i)
            return carry
        lax.fori_loop(lo, hi, run, 0)

    barrier = pltpu.get_barrier_semaphore()

    def greet(where):
        pl.semaphore_signal(barrier, inc=1, device_id=where, device_id_type=MESH)

    loads = [
        pltpu.make_async_copy(source, target, in_sem.at[i])
        for i, (source, target) in enumerate(
            ((sh_in, sh), (gain_in, gain), (labels_in, labels), (align_in, align), (mask_in, mask))
        )
    ]
    for load in loads:
        load.start()
    for c in range(C):
        pltpu.make_async_copy(tw.at[c * fc:(c + 1) * fc], twv.at[c], tw_sem.at[c]).start()
        pltpu.make_async_copy(th.at[:, c * fc:(c + 1) * fc], tbuf.at[c, me], own_sem.at[c]).start()
    sw_copy = pltpu.make_async_copy(sw, wbuf.at[pl.ds(pl.multiple_of(t * F, F), F)], sw_sem)
    sw_copy.start()

    each(1, VS, lambda k: greet(vs_peer(k)[0]))
    each(1, T, lambda k: greet(did(tt=lax.rem(t + k, T))))
    greet(did(gg=1 - g))
    pl.semaphore_wait(barrier, VS - 1 + T - 1 + 1)

    def go_left(o, c, src):
        return remote(src, tbuf.at[c, o * S + s], left_send.at[o, c], z_recv.at[o, c], did(vv=v - 1))

    def go_right(o, c, src):
        return remote(src, tbuf.at[c, o * S + s], right_send.at[o, c], z_recv.at[o, c], did(vv=v + 1))

    def go_sib(o, c, src):
        return remote(src, tbuf.at[c, o * S + s], sib_send.at[o, c], s_recv.at[o, c], did(ss=1 - s))

    for c in range(C):
        own = th.at[:, c * fc:(c + 1) * fc]

        @pl.when(v > 0)
        def _():
            go_left(v, c, own).start()

        @pl.when(v < V - 1)
        def _():
            go_right(v, c, own).start()

    def w_at(tt, hh, cw):
        return wbuf.at[pl.ds(pl.multiple_of(tt * F + hh * half + cw * wc, wc), wc)]

    def go_x(k, cw):
        to = lax.rem(t + k, T)
        src = sw.at[pl.ds(pl.multiple_of(g * half + cw * wc, wc), wc)]
        return remote(src, w_at(t, g, cw), x_send.at[to, cw], x_recv.at[t, cw], did(tt=to))

    def go_y(tt, cw):
        return remote(w_at(tt, g, cw), w_at(tt, g, cw), y_send.at[tt, cw], y_recv.at[tt, cw], did(gg=1 - g))

    def x_wait(tt, cw):
        remote(w_at(tt, g, cw), w_at(tt, g, cw), x_send.at[tt, cw], x_recv.at[tt, cw], did(tt=tt)).wait_recv()

    def y_wait(tt, cw):
        remote(w_at(tt, 1 - g, cw), w_at(tt, 1 - g, cw), y_send.at[tt, cw], y_recv.at[tt, cw], did(gg=1 - g)).wait_recv()

    nev = (T - 1) * CW
    each(0, nev, lambda j: go_x(j // CW + 1, lax.rem(j, CW)).start())
    for c in range(C):
        go_sib(v, c, th.at[:, c * fc:(c + 1) * fc]).start()

    def pass_on(j):
        tt = lax.rem(t + T - 1 - j // CW, T)
        cw = lax.rem(j, CW)
        x_wait(tt, cw)
        go_y(tt, cw).start()

    for load in loads:
        load.wait()
    hid = sh[...].astype(jnp.float32)
    inverse = lax.rsqrt(jnp.mean(hid * hid, axis=1, keepdims=True) + epsilon)
    normed[...] = (hid * inverse * gain[...]).astype(jnp.bfloat16)

    def multiply(o, c):
        x = tbuf[c, pl.ds(o * S, S)].reshape(S * rows, fc)
        acc[o] += jnp.dot(x, twv[c], preferred_element_type=jnp.float32)

    def go_acc(o):
        to = o // per
        return remote(acc.at[o], tin.at[t, lax.rem(o, per)], acc_send.at[o], acc_recv.at[t, lax.rem(o, per)], did(tt=to))

    def finished(o):
        @pl.when(o // per != t)
        def _():
            go_acc(o).start()

    acc[...] = jnp.zeros_like(acc)

    def own_chunk(c):
        pltpu.make_async_copy(tbuf.at[c, me], tbuf.at[c, me], own_sem.at[c]).wait()
        pltpu.make_async_copy(twv.at[c], twv.at[c], tw_sem.at[c]).wait()
        other = tbuf.at[c, v * S + 1 - s]
        remote(other, other, sib_send.at[v, c], s_recv.at[v, c], did(ss=1 - s)).wait_recv()
        multiply(v, c)

    each(0, C, own_chunk)
    finished(v)

    def take(o, c, onward, has_next):
        here = tbuf.at[c, o * S + s]
        remote(here, here, sib_send.at[o, c], z_recv.at[o, c], did(ss=1 - s)).wait_recv()

        @pl.when(has_next)
        def _():
            onward(o, c, here).start()

        go_sib(o, c, here).start()

    def use(o, c):
        other = tbuf.at[c, o * S + 1 - s]
        remote(other, other, sib_send.at[o, c], s_recv.at[o, c], did(ss=1 - s)).wait_recv()
        multiply(o, c)

        @pl.when(c == C - 1)
        def _():
            finished(o)

    steps = (V - 1) * C
    stride = max(1, (steps - 2) // nev)

    def step(i):
        k, c = i // C + 1, lax.rem(i, C)

        @pl.when(i < steps)
        def _():
            @pl.when(v + k < V)
            def _():
                take(v + k, c, go_left, v > 0)

            @pl.when(v - k >= 0)
            def _():
                take(v - k, c, go_right, v < V - 1)

        j = i // stride - 1

        @pl.when((lax.rem(i, stride) == 0) & (j >= 0) & (j < nev))
        def _():
            pass_on(j)

        @pl.when(i > 0)
        def _():
            kk, cc = (i - 1) // C + 1, lax.rem(i - 1, C)

            @pl.when(v + kk < V)
            def _():
                use(v + kk, cc)

            @pl.when(v - kk >= 0)
            def _():
                use(v - kk, cc)

    each(0, steps + 1, step)
    each(min(nev, steps // stride), nev, pass_on)

    sw_copy.wait()

    def y_in(j):
        y_wait(lax.rem(t + T - 1 - j // CW, T), lax.rem(j, CW))

    each(0, nev, y_in)
    student = jnp.dot(normed[...], wbuf[...], preferred_element_type=jnp.float32)
    lane_n = lax.broadcasted_iota(jnp.int32, (frames, N), 1)
    lane = lax.broadcasted_iota(jnp.int32, (frames, frames), 1)
    sub = lax.broadcasted_iota(jnp.int32, (frames, frames), 0)

    def to_columns(row):
        return jnp.transpose(jnp.broadcast_to(row, (frames, frames)))

    label_col = to_columns(labels[...].astype(jnp.float32)).astype(jnp.int32)[:, 0:1]
    onehot = (label_col - me * N) == lane_n
    label_logit = jnp.sum(jnp.where(onehot, student, 0.0), axis=1, keepdims=True)
    top_s = jnp.max(student, axis=1, keepdims=True)
    sum_s = jnp.sum(jnp.exp(student - top_s), axis=1, keepdims=True)
    align_cols = to_columns(align[...].astype(jnp.float32)).astype(jnp.int32) - t * frames
    pick = (align_cols == lane).astype(jnp.bfloat16)

    def tin_wait(j):
        tt, p = lax.rem(t + 1 + j // per, T), lax.rem(j, per)
        remote(tin.at[tt, p], tin.at[tt, p], acc_send.at[0], acc_recv.at[tt, p], did(tt=tt)).wait_recv()

    each(0, (T - 1) * per, tin_wait)
    for p in range(per):
        total = acc[t * per + p]
        for k in range(1, T):
            total = total + tin[lax.rem(t + k, T), p]
        bl[p * S * rows:(p + 1) * S * rows, :] = total
    whole = bl[...]
    hi = whole.astype(jnp.bfloat16)
    rest = whole - hi.astype(jnp.float32)
    mid = rest.astype(jnp.bfloat16)
    low = (rest - mid.astype(jnp.float32)).astype(jnp.bfloat16)
    rows_of = lambda piece: jnp.dot(pick, piece, preferred_element_type=jnp.float32)
    aligned = (rows_of(low) + rows_of(mid)) + rows_of(hi)
    top_t = jnp.max(aligned, axis=1, keepdims=True)
    exp_t = jnp.exp(aligned - top_t)
    sum_t = jnp.sum(exp_t, axis=1, keepdims=True)
    cross_t = jnp.sum(exp_t * (aligned - student), axis=1, keepdims=True)

    packed = jnp.zeros((frames, frames), jnp.float32)
    for i, column in enumerate((top_t, sum_t, cross_t, top_s, sum_s, label_logit)):
        packed = jnp.where(lane == i, column, packed)
    stats[me] = jnp.transpose(packed)[0:8, :]

    def go_stat(k):
        where, other = vs_peer(k)
        return remote(stats.at[me], stats.at[me], stat_send.at[other], stat_recv.at[me], where)

    each(1, VS, lambda k: go_stat(k).start())

    def stat_wait(k):
        where, other = vs_peer(k)
        remote(stats.at[other], stats.at[other], stat_send.at[other], stat_recv.at[other], where).wait_recv()

    each(1, VS, stat_wait)
    st = stats[...]
    row = lambda i: st[:, i, :]
    all_t = jnp.max(row(0), axis=0, keepdims=True)
    all_s = jnp.max(row(3), axis=0, keepdims=True)
    scale_t = jnp.exp(row(0) - all_t)
    scale_s = jnp.exp(row(3) - all_s)
    add = lambda x: jnp.sum(x, axis=0, keepdims=True)
    total_t = add(row(1) * scale_t)
    lse_t = all_t + jnp.log(total_t)
    lse_s = all_s + jnp.log(add(row(4) * scale_s))
    diverge = add(row(2) * scale_t) / total_t - lse_t + lse_s
    cross_term = lse_s - add(row(5))
    mask_float = mask[...].astype(jnp.float32)
    mask_count = jnp.sum(jnp.sum(mask_float, axis=1, keepdims=True), axis=0, keepdims=True)
    own_mask = mask[pl.ds(t, 1), :].astype(jnp.float32)
    row_weight = own_mask * (T * frames) / mask_count
    rl_out[...] = row_weight * (diverge + label_weight * cross_term)

    unpacked = jnp.where(sub == 0, lse_t, jnp.where(sub == 1, lse_s, row_weight))
    columns = jnp.transpose(unpacked)
    teacher_prob = jnp.exp(aligned - columns[:, 0:1])
    student_prob = jnp.exp(student - columns[:, 1:2])
    grad = (
        loss_scale * columns[:, 2:3]
        * ((1.0 + label_weight) * student_prob - teacher_prob - label_weight * onehot.astype(jnp.float32))
    ).astype(jnp.bfloat16)
    lg_out[...] = grad
    stores = [
        pltpu.make_async_copy(source, target, out_sem.at[i])
        for i, (source, target) in enumerate(((rl_out, rl_hbm), (lg_out, lg_hbm), (hg_out, hg_hbm)))
    ]
    stores[0].start()
    stores[1].start()

    inner_acc[...] = jnp.zeros_like(inner_acc)

    def term(block):
        at = pl.multiple_of(block * w, w)
        value = lax.dot_general(
            lg_out[...], wbuf[pl.ds(at, w), :], (((1,), (1,)), ((), ())), preferred_element_type=jnp.float32
        )
        weighted = value * gain[:, pl.ds(at, w)] * sh[:, pl.ds(at, w)].astype(jnp.float32)
        inner_acc[...] += jnp.sum(weighted, axis=1, keepdims=True)
        return value

    def go_gs(b):
        return remote(sibout.at[b], sibin.at[b], gs_send.at[b], gs_recv.at[b], did(ss=1 - s))

    def order(q):
        return lax.rem(q, 2) * (q // 2) + (1 - lax.rem(q, 2)) * (V - 1 - q // 2)

    def for_sib(q):
        b = order(q)
        sibout[b] = term(b * S + 1 - s)
        go_gs(b).start()

    def for_own(q):
        b = order(q)
        part[b] = term(b * S + s)

    each(0, V, for_sib)
    each(0, V, for_own)
    inner_in[me] = jnp.transpose(jnp.broadcast_to(inner_acc[...], (frames, frames)))[0:8, :]

    def go_inner(k):
        where, other = vs_peer(k)
        return remote(inner_in.at[me], inner_in.at[me], inner_send.at[other], inner_recv.at[me], where)

    each(1, VS, lambda k: go_inner(k).start())

    def piece(buf, b, p):
        return buf.at[b, pl.ds(pl.multiple_of(p * rp, rp), rp)]

    def go_line(buf, recv, b, p, onward):
        return remote(piece(part, b, p), piece(buf, b, p), ln_send.at[b, p], recv.at[b, p], did(vv=onward))

    def line(n, buf, recv, b_of, comes, onward):
        q, p = n // RP, lax.rem(n, RP)
        b = b_of(q)

        @pl.when(p == 0)
        def _():
            go_gs(b).wait_recv()
            part[b] += sibin[b]

        @pl.when(comes)
        def _():
            at = pl.ds(pl.multiple_of(p * rp, rp), rp)
            go_line(buf, recv, b, p, onward).wait_recv()
            part[b, at] += buf[b, at]

        @pl.when(n >= WIN)
        def _():
            go_line(buf, recv, b_of((n - WIN) // RP), lax.rem(n - WIN, RP), onward).wait_send()

        go_line(buf, recv, b, p, onward).start()

    from_top, from_zero = (lambda q: V - 1 - q), (lambda q: q)

    def line_step(i):
        n = i - v * LAG

        @pl.when((n >= 0) & (n < (V - 1 - v) * RP))
        def _():
            line(n, rin, r_recv, from_top, v > 0, v + 1)

        m = i - (V - 1 - v) * LAG

        @pl.when((m >= 0) & (m < v * RP))
        def _():
            line(m, lin, l_recv, from_zero, v < V - 1, v - 1)

    each(0, (V - 1) * max(RP, LAG), line_step)

    def inner_wait(k):
        where, other = vs_peer(k)
        remote(inner_in.at[other], inner_in.at[other], inner_send.at[other], inner_recv.at[other], where).wait_recv()

    each(1, VS, inner_wait)
    inner_total = jnp.sum(inner_in[...], axis=0)[0:1, :]
    inner_rows = to_columns(inner_total)[:, 0:1]

    go_gs(v).wait_recv()
    part[v] += sibin[v]

    def last(buf, recv, onward):
        each(0, RP, lambda p: go_line(buf, recv, v, p, onward).wait_recv())
        part[v] += buf[v]

    @pl.when(v > 0)
    def _():
        last(rin, r_recv, v - 1)

    @pl.when(v < V - 1)
    def _():
        last(lin, l_recv, v + 1)

    mine = pl.multiple_of(me * w, w)
    scaled = part[v] * gain[:, pl.ds(mine, w)]
    own_hidden = sh[:, pl.ds(mine, w)].astype(jnp.float32)
    hg_out[...] = (inverse * scaled - own_hidden * (inverse**3 * inner_rows / DS)).astype(jnp.bfloat16)

    stores[2].start()

    def sent(i):
        o, c = i // C, lax.rem(i, C)
        here = tbuf.at[c, o * S + s]

        @pl.when((o >= v) & (v > 0))
        def _():
            go_left(o, c, here).wait_send()

        @pl.when((o <= v) & (v < V - 1))
        def _():
            go_right(o, c, here).wait_send()

        go_sib(o, c, here).wait_send()

    each(0, V * C, sent)

    def w_sent(j):
        go_x(j // CW + 1, lax.rem(j, CW)).wait_send()
        go_y(lax.rem(t + T - 1 - j // CW, T), lax.rem(j, CW)).wait_send()

    each(0, nev, w_sent)

    def acc_sent(o):
        @pl.when(o // per != t)
        def _():
            go_acc(o).wait_send()

        go_gs(o).wait_send()

    def line_sent(j):
        @pl.when(v < V - 1)
        def _():
            n = (V - 1 - v) * RP - WIN + j
            go_line(rin, r_recv, from_top(n // RP), lax.rem(n, RP), v + 1).wait_send()

        @pl.when(v > 0)
        def _():
            n = v * RP - WIN + j
            go_line(lin, l_recv, n // RP, lax.rem(n, RP), v - 1).wait_send()

    each(0, WIN, line_sent)
    each(0, V, acc_sent)

    def small_sent(k):
        go_stat(k).wait_send()
        go_inner(k).wait_send()

    each(1, VS, small_sent)
    for store in stores:
        store.wait()


def local(sizes, teacher_hidden, teacher_weight, student_hidden, student_gain, student_weight, labels, alignment, loss_mask):
    G, V, T, S, C, CW, RP, WIN, LAG = sizes
    VS = V * S
    rows, width = teacher_hidden.shape
    fc = width // C
    N = teacher_weight.shape[1]
    frames, DS = student_hidden.shape
    w = DS // VS
    per = V // T
    f32, bf16 = jnp.float32, jnp.bfloat16
    dma = pltpu.SemaphoreType.DMA
    hbm = pl.BlockSpec(memory_space=pl.ANY)
    row_loss, logit_grad, hidden_grad = pl.pallas_call(
        functools.partial(kernel, sizes),
        out_shape=(
            jax.ShapeDtypeStruct((1, frames), f32),
            jax.ShapeDtypeStruct((frames, N), bf16),
            jax.ShapeDtypeStruct((frames, w), bf16),
        ),
        in_specs=[hbm] * 8,
        out_specs=(hbm, hbm, hbm),
        scratch_shapes=[
            pltpu.VMEM((frames, DS), bf16),
            pltpu.VMEM((1, DS), f32),
            pltpu.VMEM((1, frames), jnp.int32),
            pltpu.VMEM((1, frames), jnp.int32),
            pltpu.VMEM((T, frames), jnp.int32),
            pltpu.VMEM((1, frames), f32),
            pltpu.VMEM((frames, N), bf16),
            pltpu.VMEM((frames, w), bf16),
            pltpu.VMEM((C, VS, rows, fc), bf16),
            pltpu.VMEM((C, fc, N), bf16),
            pltpu.VMEM((DS, N), bf16),
            pltpu.VMEM((frames, DS), bf16),
            pltpu.VMEM((V, S * rows, N), f32),
            pltpu.VMEM((T, per, S * rows, N), f32),
            pltpu.VMEM((frames, N), f32),
            pltpu.VMEM((VS, 8, frames), f32),
            pltpu.VMEM((VS, 8, frames), f32),
            pltpu.VMEM((V, frames, w), f32),
            pltpu.VMEM((V, frames, w), f32),
            pltpu.VMEM((V, frames, w), f32),
            pltpu.VMEM((V, frames, w), f32),
            pltpu.VMEM((V, frames, w), f32),
            pltpu.VMEM((frames, 1), f32),
            dma((C,)), dma((C,)), dma, dma((5,)), dma((3,)),
            dma((V, C)), dma((V, C)), dma((V, C)), dma((V, C)), dma((V, C)),
            dma((T, CW)), dma((T, CW)), dma((T, CW)), dma((T, CW)),
            dma((V,)), dma((T, per)),
            dma((VS,)), dma((VS,)), dma((VS,)), dma((VS,)),
            dma((V,)), dma((V,)), dma((V, RP)), dma((V, RP)), dma((V, RP)),
        ],
        compiler_params=pltpu.CompilerParams(
            collective_id=0, has_side_effects=True, vmem_limit_bytes=63 * 2**20
        ),
    )(
        teacher_hidden, teacher_weight, student_hidden, student_gain.reshape(1, DS), student_weight,
        labels.reshape(1, frames), alignment.reshape(1, frames), loss_mask.reshape(T, frames),
    )
    return row_loss.reshape(frames), logit_grad, hidden_grad


def solution(mesh):
    sizes = tuple(mesh.shape[a] for a in ("groups", "vocab", "tokens", "section")) + (4, 4, 4, 2, 2)
    in_specs = (
        P(("groups", "vocab", "section"), "tokens"),
        P("tokens", ("vocab", "section")),
        P(("groups", "tokens"), None),
        P(),
        P("tokens", ("vocab", "section")),
        P(("groups", "tokens")),
        P(("groups", "tokens")),
        P("groups"),
    )
    out_specs = (
        P(("groups", "tokens")),
        P(("groups", "tokens"), ("vocab", "section")),
        P(("groups", "tokens"), ("vocab", "section")),
    )
    return jax.shard_map(
        functools.partial(local, sizes), mesh=mesh, in_specs=in_specs, out_specs=out_specs, check_vma=False
    )
```

```python
import functools

import jax
import jax.numpy as jnp
from jax import lax
from jax.experimental import pallas as pl
from jax.experimental.pallas import tpu as pltpu
from jax.sharding import PartitionSpec as P

label_weight = 0.2
loss_scale = 16.0
epsilon = 1e-05
MESH = pl.DeviceIdType.MESH


def kernel(
    sizes, th, tw, sh_in, gain_in, sw, labels_in, align_in, mask_in,
    rl_hbm, out_hbm,
    sh, gain, labels, align, mask, rl_out, lg_out, hg_out,
    tbuf, twv, wbuf, normed, acc, tin, bl, stats, inner_in, sibout, sibin, part, rin, lin, inner_acc,
    tw_sem, own_sem, sw_sem, in_sem, out_sem,
    left_send, right_send, sib_send, z_recv, s_recv,
    x_send, x_recv, y_send, y_recv,
    acc_send, acc_recv,
    stat_send, stat_recv, inner_send, inner_recv,
    gs_send, gs_recv, ln_send, r_recv, l_recv,
):
    G, V, T, S, C, CW, RP, WIN, LAG = sizes
    VS = V * S
    g, v, t, s = (lax.axis_index(a) for a in ("groups", "vocab", "tokens", "section"))
    me = v * S + s
    rows = th.shape[0]
    fc = th.shape[1] // C
    F = sw.shape[0]
    half = F // 2
    wc = half // CW
    frames, DS = sh.shape
    N = tw.shape[1]
    w = DS // VS
    per = V // T
    rp = frames // RP

    def did(gg=None, vv=None, tt=None, ss=None):
        pick = lambda a, b: b if a is None else a
        return (pick(gg, g), pick(vv, v), pick(tt, t), pick(ss, s))

    def remote(src, dst, send, recv, where):
        return pltpu.make_async_remote_copy(
            src_ref=src, dst_ref=dst, send_sem=send, recv_sem=recv,
            device_id=where, device_id_type=MESH,
        )

    def vs_peer(k):
        other = lax.rem(me + k, VS)
        return did(vv=other // S, ss=lax.rem(other, S)), other

    def each(lo, hi, body):
        def run(i, carry):
            body(i)
            return carry
        lax.fori_loop(lo, hi, run, 0)

    barrier = pltpu.get_barrier_semaphore()

    def greet(where):
        pl.semaphore_signal(barrier, inc=1, device_id=where, device_id_type=MESH)

    loads = [
        pltpu.make_async_copy(source, target, in_sem.at[i])
        for i, (source, target) in enumerate(
            ((sh_in, sh), (gain_in, gain), (labels_in, labels), (align_in, align), (mask_in, mask))
        )
    ]
    for load in loads:
        load.start()
    for c in range(C):
        pltpu.make_async_copy(tw.at[c * fc:(c + 1) * fc], twv.at[c], tw_sem.at[c]).start()
        pltpu.make_async_copy(th.at[:, c * fc:(c + 1) * fc], tbuf.at[c, me], own_sem.at[c]).start()
    sw_copy = pltpu.make_async_copy(sw, wbuf.at[pl.ds(pl.multiple_of(t * F, F), F)], sw_sem)
    sw_copy.start()

    each(1, VS, lambda k: greet(vs_peer(k)[0]))
    each(1, T, lambda k: greet(did(tt=lax.rem(t + k, T))))
    greet(did(gg=1 - g))
    pl.semaphore_wait(barrier, VS - 1 + T - 1 + 1)

    def go_left(o, c, src):
        return remote(src, tbuf.at[c, o * S + s], left_send.at[o, c], z_recv.at[o, c], did(vv=v - 1))

    def go_right(o, c, src):
        return remote(src, tbuf.at[c, o * S + s], right_send.at[o, c], z_recv.at[o, c], did(vv=v + 1))

    def go_sib(o, c, src):
        return remote(src, tbuf.at[c, o * S + s], sib_send.at[o, c], s_recv.at[o, c], did(ss=1 - s))

    for c in range(C):
        own = th.at[:, c * fc:(c + 1) * fc]

        @pl.when(v > 0)
        def _():
            go_left(v, c, own).start()

        @pl.when(v < V - 1)
        def _():
            go_right(v, c, own).start()

    def w_at(tt, hh, cw):
        return wbuf.at[pl.ds(pl.multiple_of(tt * F + hh * half + cw * wc, wc), wc)]

    def go_x(k, cw):
        to = lax.rem(t + k, T)
        src = sw.at[pl.ds(pl.multiple_of(g * half + cw * wc, wc), wc)]
        return remote(src, w_at(t, g, cw), x_send.at[to, cw], x_recv.at[t, cw], did(tt=to))

    def go_y(tt, cw):
        return remote(w_at(tt, g, cw), w_at(tt, g, cw), y_send.at[tt, cw], y_recv.at[tt, cw], did(gg=1 - g))

    def x_wait(tt, cw):
        remote(w_at(tt, g, cw), w_at(tt, g, cw), x_send.at[tt, cw], x_recv.at[tt, cw], did(tt=tt)).wait_recv()

    def y_wait(tt, cw):
        remote(w_at(tt, 1 - g, cw), w_at(tt, 1 - g, cw), y_send.at[tt, cw], y_recv.at[tt, cw], did(gg=1 - g)).wait_recv()

    nev = (T - 1) * CW
    each(0, nev, lambda j: go_x(j // CW + 1, lax.rem(j, CW)).start())
    for c in range(C):
        go_sib(v, c, th.at[:, c * fc:(c + 1) * fc]).start()

    def pass_on(j):
        tt = lax.rem(t + T - 1 - j // CW, T)
        cw = lax.rem(j, CW)
        x_wait(tt, cw)
        go_y(tt, cw).start()

    for load in loads:
        load.wait()
    hid = sh[...].astype(jnp.float32)
    inverse = lax.rsqrt(jnp.mean(hid * hid, axis=1, keepdims=True) + epsilon)
    normed[...] = (hid * inverse * gain[...]).astype(jnp.bfloat16)

    def multiply(o, c):
        x = tbuf[c, pl.ds(o * S, S)].reshape(S * rows, fc)
        acc[o] += jnp.dot(x, twv[c], preferred_element_type=jnp.float32)

    def go_acc(o):
        to = o // per
        return remote(acc.at[o], tin.at[t, lax.rem(o, per)], acc_send.at[o], acc_recv.at[t, lax.rem(o, per)], did(tt=to))

    def finished(o):
        @pl.when(o // per != t)
        def _():
            go_acc(o).start()

    acc[...] = jnp.zeros_like(acc)

    def own_chunk(c):
        pltpu.make_async_copy(tbuf.at[c, me], tbuf.at[c, me], own_sem.at[c]).wait()
        pltpu.make_async_copy(twv.at[c], twv.at[c], tw_sem.at[c]).wait()
        other = tbuf.at[c, v * S + 1 - s]
        remote(other, other, sib_send.at[v, c], s_recv.at[v, c], did(ss=1 - s)).wait_recv()
        multiply(v, c)

    each(0, C, own_chunk)
    finished(v)

    def take(o, c, onward, has_next):
        here = tbuf.at[c, o * S + s]
        remote(here, here, sib_send.at[o, c], z_recv.at[o, c], did(ss=1 - s)).wait_recv()

        @pl.when(has_next)
        def _():
            onward(o, c, here).start()

        go_sib(o, c, here).start()

    def use(o, c):
        other = tbuf.at[c, o * S + 1 - s]
        remote(other, other, sib_send.at[o, c], s_recv.at[o, c], did(ss=1 - s)).wait_recv()
        multiply(o, c)

        @pl.when(c == C - 1)
        def _():
            finished(o)

    steps = (V - 1) * C
    stride = max(1, (steps - 2) // nev)

    def step(i):
        k, c = i // C + 1, lax.rem(i, C)

        @pl.when(i < steps)
        def _():
            @pl.when(v + k < V)
            def _():
                take(v + k, c, go_left, v > 0)

            @pl.when(v - k >= 0)
            def _():
                take(v - k, c, go_right, v < V - 1)

        j = i // stride - 1

        @pl.when((lax.rem(i, stride) == 0) & (j >= 0) & (j < nev))
        def _():
            pass_on(j)

        @pl.when(i > 0)
        def _():
            kk, cc = (i - 1) // C + 1, lax.rem(i - 1, C)

            @pl.when(v + kk < V)
            def _():
                use(v + kk, cc)

            @pl.when(v - kk >= 0)
            def _():
                use(v - kk, cc)

    each(0, steps + 1, step)
    each(min(nev, steps // stride), nev, pass_on)

    sw_copy.wait()

    def y_in(j):
        y_wait(lax.rem(t + T - 1 - j // CW, T), lax.rem(j, CW))

    each(0, nev, y_in)
    student = jnp.dot(normed[...], wbuf[...], preferred_element_type=jnp.float32)
    lane_n = lax.broadcasted_iota(jnp.int32, (frames, N), 1)
    lane = lax.broadcasted_iota(jnp.int32, (frames, frames), 1)
    sub = lax.broadcasted_iota(jnp.int32, (frames, frames), 0)

    def to_columns(row):
        return jnp.transpose(jnp.broadcast_to(row, (frames, frames)))

    label_col = to_columns(labels[...].astype(jnp.float32)).astype(jnp.int32)[:, 0:1]
    onehot = (label_col - me * N) == lane_n
    label_logit = jnp.sum(jnp.where(onehot, student, 0.0), axis=1, keepdims=True)
    top_s = jnp.max(student, axis=1, keepdims=True)
    sum_s = jnp.sum(jnp.exp(student - top_s), axis=1, keepdims=True)
    align_cols = to_columns(align[...].astype(jnp.float32)).astype(jnp.int32) - t * frames
    pick = (align_cols == lane).astype(jnp.bfloat16)

    def tin_wait(j):
        tt, p = lax.rem(t + 1 + j // per, T), lax.rem(j, per)
        remote(tin.at[tt, p], tin.at[tt, p], acc_send.at[0], acc_recv.at[tt, p], did(tt=tt)).wait_recv()

    each(0, (T - 1) * per, tin_wait)
    for p in range(per):
        total = acc[t * per + p]
        for k in range(1, T):
            total = total + tin[lax.rem(t + k, T), p]
        bl[p * S * rows:(p + 1) * S * rows, :] = total
    whole = bl[...]
    hi = whole.astype(jnp.bfloat16)
    rest = whole - hi.astype(jnp.float32)
    mid = rest.astype(jnp.bfloat16)
    low = (rest - mid.astype(jnp.float32)).astype(jnp.bfloat16)
    rows_of = lambda piece: jnp.dot(pick, piece, preferred_element_type=jnp.float32)
    aligned = (rows_of(low) + rows_of(mid)) + rows_of(hi)
    top_t = jnp.max(aligned, axis=1, keepdims=True)
    exp_t = jnp.exp(aligned - top_t)
    sum_t = jnp.sum(exp_t, axis=1, keepdims=True)
    cross_t = jnp.sum(exp_t * (aligned - student), axis=1, keepdims=True)

    packed = jnp.zeros((frames, frames), jnp.float32)
    for i, column in enumerate((top_t, sum_t, cross_t, top_s, sum_s, label_logit)):
        packed = jnp.where(lane == i, column, packed)
    stats[me] = jnp.transpose(packed)[0:8, :]

    def go_stat(k):
        where, other = vs_peer(k)
        return remote(stats.at[me], stats.at[me], stat_send.at[other], stat_recv.at[me], where)

    each(1, VS, lambda k: go_stat(k).start())

    def stat_wait(k):
        where, other = vs_peer(k)
        remote(stats.at[other], stats.at[other], stat_send.at[other], stat_recv.at[other], where).wait_recv()

    each(1, VS, stat_wait)
    st = stats[...]
    row = lambda i: st[:, i, :]
    all_t = jnp.max(row(0), axis=0, keepdims=True)
    all_s = jnp.max(row(3), axis=0, keepdims=True)
    scale_t = jnp.exp(row(0) - all_t)
    scale_s = jnp.exp(row(3) - all_s)
    add = lambda x: jnp.sum(x, axis=0, keepdims=True)
    total_t = add(row(1) * scale_t)
    lse_t = all_t + jnp.log(total_t)
    lse_s = all_s + jnp.log(add(row(4) * scale_s))
    diverge = add(row(2) * scale_t) / total_t - lse_t + lse_s
    cross_term = lse_s - add(row(5))
    mask_float = mask[...].astype(jnp.float32)
    mask_count = jnp.sum(jnp.sum(mask_float, axis=1, keepdims=True), axis=0, keepdims=True)
    own_mask = mask[pl.ds(t, 1), :].astype(jnp.float32)
    row_weight = own_mask * (T * frames) / mask_count
    rl_out[...] = row_weight * (diverge + label_weight * cross_term)

    unpacked = jnp.where(sub == 0, lse_t, jnp.where(sub == 1, lse_s, row_weight))
    columns = jnp.transpose(unpacked)
    teacher_prob = jnp.exp(aligned - columns[:, 0:1])
    student_prob = jnp.exp(student - columns[:, 1:2])
    grad = (
        loss_scale * columns[:, 2:3]
        * ((1.0 + label_weight) * student_prob - teacher_prob - label_weight * onehot.astype(jnp.float32))
    ).astype(jnp.bfloat16)
    lg_out[...] = grad
    stores = [
        pltpu.make_async_copy(source, target, out_sem.at[i])
        for i, (source, target) in enumerate((
            (rl_out, rl_hbm),
            (lg_out, out_hbm.at[:, 0:N]),
            (hg_out, out_hbm.at[:, N:]),
        ))
    ]
    stores[0].start()
    stores[1].start()

    inner_acc[...] = jnp.zeros_like(inner_acc)

    def term(block):
        at = pl.multiple_of(block * w, w)
        value = lax.dot_general(
            lg_out[...], wbuf[pl.ds(at, w), :], (((1,), (1,)), ((), ())), preferred_element_type=jnp.float32
        )
        weighted = value * gain[:, pl.ds(at, w)] * sh[:, pl.ds(at, w)].astype(jnp.float32)
        inner_acc[...] += jnp.sum(weighted, axis=1, keepdims=True)
        return value

    def go_gs(b):
        return remote(sibout.at[b], sibin.at[b], gs_send.at[b], gs_recv.at[b], did(ss=1 - s))

    def order(q):
        return lax.rem(q, 2) * (q // 2) + (1 - lax.rem(q, 2)) * (V - 1 - q // 2)

    def for_sib(q):
        b = order(q)
        sibout[b] = term(b * S + 1 - s)
        go_gs(b).start()

    def for_own(q):
        b = order(q)
        part[b] = term(b * S + s)

    def piece(buf, b, p):
        return buf.at[b, pl.ds(pl.multiple_of(p * rp, rp), rp)]

    def go_line(buf, recv, b, p, onward):
        return remote(piece(part, b, p), piece(buf, b, p), ln_send.at[b, p], recv.at[b, p], did(vv=onward))

    def line(n, buf, recv, b_of, comes, onward):
        q, p = n // RP, lax.rem(n, RP)
        b = b_of(q)

        @pl.when(p == 0)
        def _():
            go_gs(b).wait_recv()
            part[b] += sibin[b]

        @pl.when(comes)
        def _():
            at = pl.ds(pl.multiple_of(p * rp, rp), rp)
            go_line(buf, recv, b, p, onward).wait_recv()
            part[b, at] += buf[b, at]

        @pl.when(n >= WIN)
        def _():
            go_line(buf, recv, b_of((n - WIN) // RP), lax.rem(n - WIN, RP), onward).wait_send()

        go_line(buf, recv, b, p, onward).start()

    from_top, from_zero = (lambda q: V - 1 - q), (lambda q: q)

    def line_step(i):
        n = i - v * LAG

        @pl.when((n >= 0) & (n < (V - 1 - v) * RP))
        def _():
            line(n, rin, r_recv, from_top, v > 0, v + 1)

        m = i - (V - 1 - v) * LAG

        @pl.when((m >= 0) & (m < v * RP))
        def _():
            line(m, lin, l_recv, from_zero, v < V - 1, v - 1)

    each(0, 2, for_sib)
    each(0, 2, for_own)
    each(0, LAG, line_step)
    each(2, V, for_sib)
    each(2, V, for_own)
    inner_in[me] = jnp.transpose(jnp.broadcast_to(inner_acc[...], (frames, frames)))[0:8, :]

    def go_inner(k):
        where, other = vs_peer(k)
        return remote(inner_in.at[me], inner_in.at[me], inner_send.at[other], inner_recv.at[me], where)

    each(1, VS, lambda k: go_inner(k).start())
    each(LAG, (V - 1) * max(RP, LAG), line_step)

    def inner_wait(k):
        where, other = vs_peer(k)
        remote(inner_in.at[other], inner_in.at[other], inner_send.at[other], inner_recv.at[other], where).wait_recv()

    each(1, VS, inner_wait)
    inner_total = jnp.sum(inner_in[...], axis=0)[0:1, :]
    inner_rows = to_columns(inner_total)[:, 0:1]

    go_gs(v).wait_recv()
    part[v] += sibin[v]

    def last(buf, recv, onward):
        each(0, RP, lambda p: go_line(buf, recv, v, p, onward).wait_recv())
        part[v] += buf[v]

    @pl.when(v > 0)
    def _():
        last(rin, r_recv, v - 1)

    @pl.when(v < V - 1)
    def _():
        last(lin, l_recv, v + 1)

    mine = pl.multiple_of(me * w, w)
    scaled = part[v] * gain[:, pl.ds(mine, w)]
    own_hidden = sh[:, pl.ds(mine, w)].astype(jnp.float32)
    hg_out[...] = (inverse * scaled - own_hidden * (inverse**3 * inner_rows / DS)).astype(jnp.bfloat16)

    stores[2].start()

    def sent(i):
        o, c = i // C, lax.rem(i, C)
        here = tbuf.at[c, o * S + s]

        @pl.when((o >= v) & (v > 0))
        def _():
            go_left(o, c, here).wait_send()

        @pl.when((o <= v) & (v < V - 1))
        def _():
            go_right(o, c, here).wait_send()

        go_sib(o, c, here).wait_send()

    each(0, V * C, sent)

    def w_sent(j):
        go_x(j // CW + 1, lax.rem(j, CW)).wait_send()
        go_y(lax.rem(t + T - 1 - j // CW, T), lax.rem(j, CW)).wait_send()

    each(0, nev, w_sent)

    def acc_sent(o):
        @pl.when(o // per != t)
        def _():
            go_acc(o).wait_send()

        go_gs(o).wait_send()

    def line_sent(j):
        @pl.when(v < V - 1)
        def _():
            n = (V - 1 - v) * RP - WIN + j
            go_line(rin, r_recv, from_top(n // RP), lax.rem(n, RP), v + 1).wait_send()

        @pl.when(v > 0)
        def _():
            n = v * RP - WIN + j
            go_line(lin, l_recv, n // RP, lax.rem(n, RP), v - 1).wait_send()

    each(0, WIN, line_sent)
    each(0, V, acc_sent)

    def small_sent(k):
        go_stat(k).wait_send()
        go_inner(k).wait_send()

    each(1, VS, small_sent)
    for store in stores:
        store.wait()


def local(sizes, teacher_hidden, teacher_weight, student_hidden, student_gain, student_weight, labels, alignment, loss_mask):
    G, V, T, S, C, CW, RP, WIN, LAG = sizes
    VS = V * S
    rows, width = teacher_hidden.shape
    fc = width // C
    N = teacher_weight.shape[1]
    frames, DS = student_hidden.shape
    w = DS // VS
    per = V // T
    f32, bf16 = jnp.float32, jnp.bfloat16
    dma = pltpu.SemaphoreType.DMA
    hbm = pl.BlockSpec(memory_space=pl.ANY)
    row_loss, both = pl.pallas_call(
        functools.partial(kernel, sizes),
        out_shape=(jax.ShapeDtypeStruct((1, frames), f32), jax.ShapeDtypeStruct((frames, N + w), bf16)),
        in_specs=[hbm] * 8,
        out_specs=(hbm, hbm),
        scratch_shapes=[
            pltpu.VMEM((frames, DS), bf16),
            pltpu.VMEM((1, DS), f32),
            pltpu.VMEM((1, frames), jnp.int32),
            pltpu.VMEM((1, frames), jnp.int32),
            pltpu.VMEM((T, frames), jnp.int32),
            pltpu.VMEM((1, frames), f32),
            pltpu.VMEM((frames, N), bf16),
            pltpu.VMEM((frames, w), bf16),
            pltpu.VMEM((C, VS, rows, fc), bf16),
            pltpu.VMEM((C, fc, N), bf16),
            pltpu.VMEM((DS, N), bf16),
            pltpu.VMEM((frames, DS), bf16),
            pltpu.VMEM((V, S * rows, N), f32),
            pltpu.VMEM((T, per, S * rows, N), f32),
            pltpu.VMEM((frames, N), f32),
            pltpu.VMEM((VS, 8, frames), f32),
            pltpu.VMEM((VS, 8, frames), f32),
            pltpu.VMEM((V, frames, w), f32),
            pltpu.VMEM((V, frames, w), f32),
            pltpu.VMEM((V, frames, w), f32),
            pltpu.VMEM((V, frames, w), f32),
            pltpu.VMEM((V, frames, w), f32),
            pltpu.VMEM((frames, 1), f32),
            dma((C,)), dma((C,)), dma, dma((5,)), dma((3,)),
            dma((V, C)), dma((V, C)), dma((V, C)), dma((V, C)), dma((V, C)),
            dma((T, CW)), dma((T, CW)), dma((T, CW)), dma((T, CW)),
            dma((V,)), dma((T, per)),
            dma((VS,)), dma((VS,)), dma((VS,)), dma((VS,)),
            dma((V,)), dma((V,)), dma((V, RP)), dma((V, RP)), dma((V, RP)),
        ],
        compiler_params=pltpu.CompilerParams(
            collective_id=0, has_side_effects=True, vmem_limit_bytes=63 * 2**20
        ),
    )(
        teacher_hidden, teacher_weight, student_hidden, student_gain.reshape(1, DS), student_weight,
        labels.reshape(1, frames), alignment.reshape(1, frames), loss_mask.reshape(T, frames),
    )
    return row_loss.reshape(frames), both[:, :N], both[:, N:]


def solution(mesh):
    sizes = tuple(mesh.shape[a] for a in ("groups", "vocab", "tokens", "section")) + (4, 4, 4, 2, 2)
    in_specs = (
        P(("groups", "vocab", "section"), "tokens"),
        P("tokens", ("vocab", "section")),
        P(("groups", "tokens"), None),
        P(),
        P("tokens", ("vocab", "section")),
        P(("groups", "tokens")),
        P(("groups", "tokens")),
        P("groups"),
    )
    out_specs = (
        P(("groups", "tokens")),
        P(("groups", "tokens"), ("vocab", "section")),
        P(("groups", "tokens"), ("vocab", "section")),
    )
    return jax.shard_map(
        functools.partial(local, sizes), mesh=mesh, in_specs=in_specs, out_specs=out_specs, check_vma=False
    )
```

```python
import functools

import jax
import jax.numpy as jnp
from jax import lax
from jax.experimental import pallas as pl
from jax.experimental.pallas import tpu as pltpu
from jax.sharding import PartitionSpec as P

label_weight = 0.2
loss_scale = 16.0
epsilon = 1e-05
MESH = pl.DeviceIdType.MESH


def kernel(
    sizes, th, tw, sh_in, gain_in, sw, labels_in, align_in, mask_in,
    rl_hbm, out_hbm,
    sh, gain, labels, align, mask, rl_out, lg_out, hg_out,
    tbuf, twv, wbuf, normed, acc, tin, bl, stats, inner_in, sibout, sibin, part, rin, lin, inner_acc,
    tw_sem, own_sem, sw_sem, in_sem, out_sem,
    left_send, right_send, sib_send, z_recv, s_recv,
    x_send, x_recv, y_send, y_recv,
    acc_send, acc_recv,
    stat_send, stat_recv, inner_send, inner_recv,
    gs_send, gs_recv, ln_send, r_recv, l_recv,
):
    G, V, T, S, C, CW, RP, WIN, LAG = sizes
    VS = V * S
    g, v, t, s = (lax.axis_index(a) for a in ("groups", "vocab", "tokens", "section"))
    me = v * S + s
    rows = th.shape[0]
    fc = th.shape[1] // C
    F = sw.shape[0]
    half = F // 2
    wc = half // CW
    frames, DS = sh.shape
    N = tw.shape[1]
    w = DS // VS
    per = V // T
    rp = frames // RP

    def did(gg=None, vv=None, tt=None, ss=None):
        pick = lambda a, b: b if a is None else a
        return (pick(gg, g), pick(vv, v), pick(tt, t), pick(ss, s))

    def remote(src, dst, send, recv, where):
        return pltpu.make_async_remote_copy(
            src_ref=src, dst_ref=dst, send_sem=send, recv_sem=recv,
            device_id=where, device_id_type=MESH,
        )

    def vs_peer(k):
        other = lax.rem(me + k, VS)
        return did(vv=other // S, ss=lax.rem(other, S)), other

    def each(lo, hi, body):
        def run(i, carry):
            body(i)
            return carry
        lax.fori_loop(lo, hi, run, 0)

    barrier = pltpu.get_barrier_semaphore()

    def greet(where):
        pl.semaphore_signal(barrier, inc=1, device_id=where, device_id_type=MESH)

    loads = [
        pltpu.make_async_copy(source, target, in_sem.at[i])
        for i, (source, target) in enumerate(
            ((sh_in, sh), (gain_in, gain), (labels_in, labels), (align_in, align), (mask_in, mask))
        )
    ]
    for load in loads:
        load.start()
    for c in range(C):
        pltpu.make_async_copy(tw.at[c * fc:(c + 1) * fc], twv.at[c], tw_sem.at[c]).start()
        pltpu.make_async_copy(th.at[:, c * fc:(c + 1) * fc], tbuf.at[c, me], own_sem.at[c]).start()
    sw_copy = pltpu.make_async_copy(sw, wbuf.at[pl.ds(pl.multiple_of(t * F, F), F)], sw_sem)
    sw_copy.start()

    each(1, VS, lambda k: greet(vs_peer(k)[0]))
    each(1, T, lambda k: greet(did(tt=lax.rem(t + k, T))))
    greet(did(gg=1 - g))
    pl.semaphore_wait(barrier, VS - 1 + T - 1 + 1)

    def go_left(o, c, src):
        return remote(src, tbuf.at[c, o * S + s], left_send.at[o, c], z_recv.at[o, c], did(vv=v - 1))

    def go_right(o, c, src):
        return remote(src, tbuf.at[c, o * S + s], right_send.at[o, c], z_recv.at[o, c], did(vv=v + 1))

    def go_sib(o, c, src):
        return remote(src, tbuf.at[c, o * S + s], sib_send.at[o, c], s_recv.at[o, c], did(ss=1 - s))

    for c in range(C):
        own = th.at[:, c * fc:(c + 1) * fc]

        @pl.when(v > 0)
        def _():
            go_left(v, c, own).start()

        @pl.when(v < V - 1)
        def _():
            go_right(v, c, own).start()

    def w_at(tt, hh, cw):
        return wbuf.at[pl.ds(pl.multiple_of(tt * F + hh * half + cw * wc, wc), wc)]

    def go_x(k, cw):
        to = lax.rem(t + k, T)
        src = sw.at[pl.ds(pl.multiple_of(g * half + cw * wc, wc), wc)]
        return remote(src, w_at(t, g, cw), x_send.at[to, cw], x_recv.at[t, cw], did(tt=to))

    def go_y(tt, cw):
        return remote(w_at(tt, g, cw), w_at(tt, g, cw), y_send.at[tt, cw], y_recv.at[tt, cw], did(gg=1 - g))

    def x_wait(tt, cw):
        remote(w_at(tt, g, cw), w_at(tt, g, cw), x_send.at[tt, cw], x_recv.at[tt, cw], did(tt=tt)).wait_recv()

    def y_wait(tt, cw):
        remote(w_at(tt, 1 - g, cw), w_at(tt, 1 - g, cw), y_send.at[tt, cw], y_recv.at[tt, cw], did(gg=1 - g)).wait_recv()

    nev = (T - 1) * CW
    each(0, nev, lambda j: go_x(j // CW + 1, lax.rem(j, CW)).start())
    for c in range(C):
        go_sib(v, c, th.at[:, c * fc:(c + 1) * fc]).start()

    def pass_on(j):
        tt = lax.rem(t + T - 1 - j // CW, T)
        cw = lax.rem(j, CW)
        x_wait(tt, cw)
        go_y(tt, cw).start()

    for load in loads:
        load.wait()
    hid = sh[...].astype(jnp.float32)
    inverse = lax.rsqrt(jnp.mean(hid * hid, axis=1, keepdims=True) + epsilon)
    normed[...] = (hid * inverse * gain[...]).astype(jnp.bfloat16)

    def multiply(o, c):
        x = tbuf[c, pl.ds(o * S, S)].reshape(S * rows, fc)
        acc[o] += jnp.dot(x, twv[c], preferred_element_type=jnp.float32)

    def go_acc(o):
        to = o // per
        return remote(acc.at[o], tin.at[t, lax.rem(o, per)], acc_send.at[o], acc_recv.at[t, lax.rem(o, per)], did(tt=to))

    def finished(o):
        @pl.when(o // per != t)
        def _():
            go_acc(o).start()

    acc[...] = jnp.zeros_like(acc)

    def own_chunk(c):
        pltpu.make_async_copy(tbuf.at[c, me], tbuf.at[c, me], own_sem.at[c]).wait()
        pltpu.make_async_copy(twv.at[c], twv.at[c], tw_sem.at[c]).wait()
        other = tbuf.at[c, v * S + 1 - s]
        remote(other, other, sib_send.at[v, c], s_recv.at[v, c], did(ss=1 - s)).wait_recv()
        multiply(v, c)

    each(0, C, own_chunk)
    finished(v)

    def take(o, c, onward, has_next):
        here = tbuf.at[c, o * S + s]
        remote(here, here, sib_send.at[o, c], z_recv.at[o, c], did(ss=1 - s)).wait_recv()

        @pl.when(has_next)
        def _():
            onward(o, c, here).start()

        go_sib(o, c, here).start()

    def use(o, c):
        other = tbuf.at[c, o * S + 1 - s]
        remote(other, other, sib_send.at[o, c], s_recv.at[o, c], did(ss=1 - s)).wait_recv()
        multiply(o, c)

        @pl.when(c == C - 1)
        def _():
            finished(o)

    steps = (V - 1) * C
    stride = max(1, (steps - 2) // nev)

    def step(i):
        k, c = i // C + 1, lax.rem(i, C)

        @pl.when(i < steps)
        def _():
            @pl.when(v + k < V)
            def _():
                take(v + k, c, go_left, v > 0)

            @pl.when(v - k >= 0)
            def _():
                take(v - k, c, go_right, v < V - 1)

        j = i // stride - 1

        @pl.when((lax.rem(i, stride) == 0) & (j >= 0) & (j < nev))
        def _():
            pass_on(j)

        @pl.when(i > 0)
        def _():
            kk, cc = (i - 1) // C + 1, lax.rem(i - 1, C)

            @pl.when(v + kk < V)
            def _():
                use(v + kk, cc)

            @pl.when(v - kk >= 0)
            def _():
                use(v - kk, cc)

    each(0, steps + 1, step)
    each(min(nev, steps // stride), nev, pass_on)

    sw_copy.wait()

    def y_in(j):
        y_wait(lax.rem(t + T - 1 - j // CW, T), lax.rem(j, CW))

    each(0, nev, y_in)
    student = jnp.dot(normed[...], wbuf[...], preferred_element_type=jnp.float32)
    lane_n = lax.broadcasted_iota(jnp.int32, (frames, N), 1)
    lane = lax.broadcasted_iota(jnp.int32, (frames, frames), 1)
    sub = lax.broadcasted_iota(jnp.int32, (frames, frames), 0)

    def to_columns(row):
        return jnp.transpose(jnp.broadcast_to(row, (frames, frames)))

    label_col = to_columns(labels[...].astype(jnp.float32)).astype(jnp.int32)[:, 0:1]
    onehot = (label_col - me * N) == lane_n
    label_logit = jnp.sum(jnp.where(onehot, student, 0.0), axis=1, keepdims=True)
    top_s = jnp.max(student, axis=1, keepdims=True)
    sum_s = jnp.sum(jnp.exp(student - top_s), axis=1, keepdims=True)
    align_cols = to_columns(align[...].astype(jnp.float32)).astype(jnp.int32) - t * frames
    pick = (align_cols == lane).astype(jnp.bfloat16)

    def tin_wait(j):
        tt, p = lax.rem(t + 1 + j // per, T), lax.rem(j, per)
        remote(tin.at[tt, p], tin.at[tt, p], acc_send.at[0], acc_recv.at[tt, p], did(tt=tt)).wait_recv()

    each(0, (T - 1) * per, tin_wait)
    for p in range(per):
        total = acc[t * per + p]
        for k in range(1, T):
            total = total + tin[lax.rem(t + k, T), p]
        bl[p * S * rows:(p + 1) * S * rows, :] = total
    whole = bl[...]
    hi = whole.astype(jnp.bfloat16)
    rest = whole - hi.astype(jnp.float32)
    mid = rest.astype(jnp.bfloat16)
    low = (rest - mid.astype(jnp.float32)).astype(jnp.bfloat16)
    rows_of = lambda piece: jnp.dot(pick, piece, preferred_element_type=jnp.float32)
    aligned = (rows_of(low) + rows_of(mid)) + rows_of(hi)
    top_t = jnp.max(aligned, axis=1, keepdims=True)
    exp_t = jnp.exp(aligned - top_t)
    sum_t = jnp.sum(exp_t, axis=1, keepdims=True)
    cross_t = jnp.sum(exp_t * (aligned - student), axis=1, keepdims=True)

    packed = jnp.zeros((frames, frames), jnp.float32)
    for i, column in enumerate((top_t, sum_t, cross_t, top_s, sum_s, label_logit)):
        packed = jnp.where(lane == i, column, packed)
    stats[me] = jnp.transpose(packed)[0:8, :]

    def go_stat(k):
        where, other = vs_peer(k)
        return remote(stats.at[me], stats.at[me], stat_send.at[other], stat_recv.at[me], where)

    each(1, VS, lambda k: go_stat(k).start())

    def stat_wait(k):
        where, other = vs_peer(k)
        remote(stats.at[other], stats.at[other], stat_send.at[other], stat_recv.at[other], where).wait_recv()

    each(1, VS, stat_wait)
    st = stats[...]
    row = lambda i: st[:, i, :]
    all_t = jnp.max(row(0), axis=0, keepdims=True)
    all_s = jnp.max(row(3), axis=0, keepdims=True)
    scale_t = jnp.exp(row(0) - all_t)
    scale_s = jnp.exp(row(3) - all_s)
    add = lambda x: jnp.sum(x, axis=0, keepdims=True)
    total_t = add(row(1) * scale_t)
    lse_t = all_t + jnp.log(total_t)
    lse_s = all_s + jnp.log(add(row(4) * scale_s))
    diverge = add(row(2) * scale_t) / total_t - lse_t + lse_s
    cross_term = lse_s - add(row(5))
    mask_float = mask[...].astype(jnp.float32)
    mask_count = jnp.sum(jnp.sum(mask_float, axis=1, keepdims=True), axis=0, keepdims=True)
    own_mask = mask[pl.ds(t, 1), :].astype(jnp.float32)
    row_weight = own_mask * (T * frames) / mask_count
    rl_out[...] = row_weight * (diverge + label_weight * cross_term)

    unpacked = jnp.where(sub == 0, lse_t, jnp.where(sub == 1, lse_s, row_weight))
    columns = jnp.transpose(unpacked)
    teacher_prob = jnp.exp(aligned - columns[:, 0:1])
    student_prob = jnp.exp(student - columns[:, 1:2])
    grad = (
        loss_scale * columns[:, 2:3]
        * ((1.0 + label_weight) * student_prob - teacher_prob - label_weight * onehot.astype(jnp.float32))
    ).astype(jnp.bfloat16)
    lg_out[...] = grad
    stores = [
        pltpu.make_async_copy(source, target, out_sem.at[i])
        for i, (source, target) in enumerate((
            (rl_out, rl_hbm),
            (lg_out, out_hbm.at[:, 0:N]),
            (hg_out, out_hbm.at[:, N:]),
        ))
    ]
    stores[0].start()
    stores[1].start()

    inner_acc[...] = jnp.zeros_like(inner_acc)

    def term(block):
        at = pl.multiple_of(block * w, w)
        value = lax.dot_general(
            lg_out[...], wbuf[pl.ds(at, w), :], (((1,), (1,)), ((), ())), preferred_element_type=jnp.float32
        )
        weighted = value * gain[:, pl.ds(at, w)] * sh[:, pl.ds(at, w)].astype(jnp.float32)
        inner_acc[...] += jnp.sum(weighted, axis=1, keepdims=True)
        return value

    def go_gs(b):
        return remote(sibout.at[b], sibin.at[b], gs_send.at[b], gs_recv.at[b], did(ss=1 - s))

    def order(q):
        return lax.rem(q, 2) * (q // 2) + (1 - lax.rem(q, 2)) * (V - 1 - q // 2)

    def for_sib(q):
        b = order(q)
        sibout[b] = term(b * S + 1 - s)
        go_gs(b).start()

    def for_own(q):
        b = order(q)
        part[b] = term(b * S + s)

    def piece(buf, b, p):
        return buf.at[b, pl.ds(pl.multiple_of(p * rp, rp), rp)]

    def go_line(buf, recv, b, p, onward):
        return remote(piece(part, b, p), piece(buf, b, p), ln_send.at[b, p], recv.at[b, p], did(vv=onward))

    def line(n, buf, recv, b_of, comes, onward):
        q, p = n // RP, lax.rem(n, RP)
        b = b_of(q)

        @pl.when(p == 0)
        def _():
            go_gs(b).wait_recv()
            part[b] += sibin[b]

        @pl.when(comes)
        def _():
            at = pl.ds(pl.multiple_of(p * rp, rp), rp)
            go_line(buf, recv, b, p, onward).wait_recv()
            part[b, at] += buf[b, at]

        @pl.when(n >= WIN)
        def _():
            go_line(buf, recv, b_of((n - WIN) // RP), lax.rem(n - WIN, RP), onward).wait_send()

        go_line(buf, recv, b, p, onward).start()

    from_top, from_zero = (lambda q: V - 1 - q), (lambda q: q)

    def line_step(i):
        n = i - v * LAG

        @pl.when((n >= 0) & (n < (V - 1 - v) * RP))
        def _():
            line(n, rin, r_recv, from_top, v > 0, v + 1)

        m = i - (V - 1 - v) * LAG

        @pl.when((m >= 0) & (m < v * RP))
        def _():
            line(m, lin, l_recv, from_zero, v < V - 1, v - 1)

    each(0, 2, for_sib)
    each(0, 2, for_own)
    each(0, LAG, line_step)
    each(2, V, for_sib)
    each(2, V, for_own)
    inner_in[me] = jnp.transpose(jnp.broadcast_to(inner_acc[...], (frames, frames)))[0:8, :]

    def go_inner(k):
        where, other = vs_peer(k)
        return remote(inner_in.at[me], inner_in.at[me], inner_send.at[other], inner_recv.at[me], where)

    each(1, VS, lambda k: go_inner(k).start())
    each(LAG, (V - 1) * max(RP, LAG), line_step)

    def inner_wait(k):
        where, other = vs_peer(k)
        remote(inner_in.at[other], inner_in.at[other], inner_send.at[other], inner_recv.at[other], where).wait_recv()

    def sent(i):
        o, c = i // C, lax.rem(i, C)
        here = tbuf.at[c, o * S + s]

        @pl.when((o >= v) & (v > 0))
        def _():
            go_left(o, c, here).wait_send()

        @pl.when((o <= v) & (v < V - 1))
        def _():
            go_right(o, c, here).wait_send()

        go_sib(o, c, here).wait_send()

    each(0, V * C, sent)

    def w_sent(j):
        go_x(j // CW + 1, lax.rem(j, CW)).wait_send()
        go_y(lax.rem(t + T - 1 - j // CW, T), lax.rem(j, CW)).wait_send()

    each(0, nev, w_sent)

    def acc_sent(o):
        @pl.when(o // per != t)
        def _():
            go_acc(o).wait_send()

        go_gs(o).wait_send()

    each(0, V, acc_sent)

    def small_sent(k):
        go_stat(k).wait_send()
        go_inner(k).wait_send()

    each(1, VS, small_sent)
    each(1, VS, inner_wait)
    inner_total = jnp.sum(inner_in[...], axis=0)[0:1, :]
    inner_rows = to_columns(inner_total)[:, 0:1]

    go_gs(v).wait_recv()
    part[v] += sibin[v]

    def last(buf, recv, onward):
        each(0, RP, lambda p: go_line(buf, recv, v, p, onward).wait_recv())
        part[v] += buf[v]

    @pl.when(v > 0)
    def _():
        last(rin, r_recv, v - 1)

    @pl.when(v < V - 1)
    def _():
        last(lin, l_recv, v + 1)

    mine = pl.multiple_of(me * w, w)
    scaled = part[v] * gain[:, pl.ds(mine, w)]
    own_hidden = sh[:, pl.ds(mine, w)].astype(jnp.float32)
    hg_out[...] = (inverse * scaled - own_hidden * (inverse**3 * inner_rows / DS)).astype(jnp.bfloat16)

    stores[2].start()

    def line_sent(j):
        @pl.when(v < V - 1)
        def _():
            n = (V - 1 - v) * RP - WIN + j
            go_line(rin, r_recv, from_top(n // RP), lax.rem(n, RP), v + 1).wait_send()

        @pl.when(v > 0)
        def _():
            n = v * RP - WIN + j
            go_line(lin, l_recv, n // RP, lax.rem(n, RP), v - 1).wait_send()

    each(0, WIN, line_sent)
    for store in stores:
        store.wait()


def local(sizes, teacher_hidden, teacher_weight, student_hidden, student_gain, student_weight, labels, alignment, loss_mask):
    G, V, T, S, C, CW, RP, WIN, LAG = sizes
    VS = V * S
    rows, width = teacher_hidden.shape
    fc = width // C
    N = teacher_weight.shape[1]
    frames, DS = student_hidden.shape
    w = DS // VS
    per = V // T
    f32, bf16 = jnp.float32, jnp.bfloat16
    dma = pltpu.SemaphoreType.DMA
    hbm = pl.BlockSpec(memory_space=pl.ANY)
    row_loss, both = pl.pallas_call(
        functools.partial(kernel, sizes),
        out_shape=(jax.ShapeDtypeStruct((1, frames), f32), jax.ShapeDtypeStruct((frames, N + w), bf16)),
        in_specs=[hbm] * 8,
        out_specs=(hbm, hbm),
        scratch_shapes=[
            pltpu.VMEM((frames, DS), bf16),
            pltpu.VMEM((1, DS), f32),
            pltpu.VMEM((1, frames), jnp.int32),
            pltpu.VMEM((1, frames), jnp.int32),
            pltpu.VMEM((T, frames), jnp.int32),
            pltpu.VMEM((1, frames), f32),
            pltpu.VMEM((frames, N), bf16),
            pltpu.VMEM((frames, w), bf16),
            pltpu.VMEM((C, VS, rows, fc), bf16),
            pltpu.VMEM((C, fc, N), bf16),
            pltpu.VMEM((DS, N), bf16),
            pltpu.VMEM((frames, DS), bf16),
            pltpu.VMEM((V, S * rows, N), f32),
            pltpu.VMEM((T, per, S * rows, N), f32),
            pltpu.VMEM((frames, N), f32),
            pltpu.VMEM((VS, 8, frames), f32),
            pltpu.VMEM((VS, 8, frames), f32),
            pltpu.VMEM((V, frames, w), f32),
            pltpu.VMEM((V, frames, w), f32),
            pltpu.VMEM((V, frames, w), f32),
            pltpu.VMEM((V, frames, w), f32),
            pltpu.VMEM((V, frames, w), f32),
            pltpu.VMEM((frames, 1), f32),
            dma((C,)), dma((C,)), dma, dma((5,)), dma((3,)),
            dma((V, C)), dma((V, C)), dma((V, C)), dma((V, C)), dma((V, C)),
            dma((T, CW)), dma((T, CW)), dma((T, CW)), dma((T, CW)),
            dma((V,)), dma((T, per)),
            dma((VS,)), dma((VS,)), dma((VS,)), dma((VS,)),
            dma((V,)), dma((V,)), dma((V, RP)), dma((V, RP)), dma((V, RP)),
        ],
        compiler_params=pltpu.CompilerParams(
            collective_id=0, has_side_effects=True, vmem_limit_bytes=63 * 2**20
        ),
    )(
        teacher_hidden, teacher_weight, student_hidden, student_gain.reshape(1, DS), student_weight,
        labels.reshape(1, frames), alignment.reshape(1, frames), loss_mask.reshape(T, frames),
    )
    return row_loss.reshape(frames), both[:, :N], both[:, N:]


def solution(mesh):
    sizes = tuple(mesh.shape[a] for a in ("groups", "vocab", "tokens", "section")) + (4, 4, 4, 2, 2)
    in_specs = (
        P(("groups", "vocab", "section"), "tokens"),
        P("tokens", ("vocab", "section")),
        P(("groups", "tokens"), None),
        P(),
        P("tokens", ("vocab", "section")),
        P(("groups", "tokens")),
        P(("groups", "tokens")),
        P("groups"),
    )
    out_specs = (
        P(("groups", "tokens")),
        P(("groups", "tokens"), ("vocab", "section")),
        P(("groups", "tokens"), ("vocab", "section")),
    )
    return jax.shard_map(
        functools.partial(local, sizes), mesh=mesh, in_specs=in_specs, out_specs=out_specs, check_vma=False
    )
```
